256 devices in a mesh: dp: 64 (over z, x, core), head: 4 (over y).
Axes of the slice: x: 4, y: 4, z: 8, core: 2. Of those that a mesh axis runs over, the one named last changes fastest.
Arguments:
- queries: bfloat16 [32768, 2048], P('dp', 'head'), may hold values from -48 to 48
- encodings: bfloat16 [1024, 128, 896], P('dp', None, 'head'), may hold values from -12 to 12
- neighbour_ids: int32 [512, 2], P('dp'), may hold values from 0 to 1023, as said below
- block_place: int32 [1024], replicated, may hold values from 0 to 1023, as said below
- query_weight: bfloat16 [4096, 2048], P(None, 'head'), may hold values from -1 to 1
- key_weight: bfloat16 [896, 2048], P(None, 'head'), may hold values from -1 to 1
- value_weight: bfloat16 [896, 2048], P(None, 'head'), may hold values from -0.1875 to 0.1875
- attn_grad: bfloat16 [32768, 2048], P('dp', 'head'), may hold values from -24 to 24
Outputs:
- query_input_grad: bfloat16 [32768, 4096], P('dp', 'head')
- encodings_grad: bfloat16 [1024, 128, 896], P('dp', None, 'head')
- key_weight_grad: float32 [896, 2048], P('dp', 'head')
- value_weight_grad: float32 [896, 2048], P('dp', 'head')
The draws below stay inside these ranges and needn't reach their ends.
Inputs may be any that keep to these rules, and one draw needn't show every extreme that they name: `neighbour_ids`: block b is stored at position block_place[b] of encodings, on the index block_place[b] // 16 of dp. Of the 16 slots of the spans of one index of dp, each index of dp stores the blocks of 1 or 0, and some index stores those of exactly 1. `block_place`: A permutation: every position once.
All inputs are finite; a program needn't handle non-finite values.
Results may differ from the reference program's by a relative error of at most 0.012.
The reference program's roundings to bfloat16 on the way count: a program that leaves them out, or rounds other values in their place, can miss the bound.
Values may be sent and summed in bfloat16 or wider, within the bound.
No kernel may reach another device: no remote copies, remote signals or barrier semaphores. Data moves between devices by JAX's collectives and lax.ppermute only.
A program may use at most 128 MiB of HBM per device.

```python
import math
import jax
import jax.numpy as jnp
from jax import lax

D = 4096
HEADS = 16
DH = 128
E = 896
CH = 64
NTOK = 128
NEIGH = 2
CH_DEV = 8
HC = 2048
SPANS = 512
TOKENS = 32768
BLK_DEV = 16
BLOCKS = 1024
N_DP = 64
N_HEAD = 4


def neighbour_plan(key):
    base = jax.random.fold_in(key, 501)
    key_order, key_first, key_second, key_names = jax.random.split(base, 4)
    slot_total = NEIGH * CH_DEV
    order = jax.vmap(lambda single: jax.random.permutation(single, N_DP))(jax.random.split(key_order, N_DP))
    owner_dev = order[:, jnp.arange(slot_total) % N_DP]
    first = jax.random.randint(key_first, (N_DP, slot_total), 0, BLK_DEV)
    second = jax.random.randint(key_second, (N_DP, slot_total), 0, BLK_DEV)
    position = (owner_dev * BLK_DEV + jnp.minimum(first, second)).astype(jnp.int32)
    id_at = jax.random.permutation(key_names, BLOCKS).astype(jnp.int32)
    place = jnp.argsort(id_at).astype(jnp.int32)
    block_names = id_at[position].reshape(SPANS, NEIGH).astype(jnp.int32)
    return (block_names, place)


def projections(key):
    key_query, key_key = jax.random.split(jax.random.fold_in(key, 502))
    query_proj = jnp.clip(jax.random.normal(key_query, (D, HEADS * DH), jnp.float32), -6.0, 6.0) / math.sqrt(D)
    key_proj = jnp.clip(jax.random.normal(key_key, (E, HEADS * DH), jnp.float32), -6.0, 6.0) / math.sqrt(E)
    return (query_proj, key_proj)


def draw_queries(key, part):
    values = jnp.clip(jax.random.normal(jax.random.fold_in(key, 504), (TOKENS, HEADS * DH), jnp.float32), -6.0, 6.0)
    return jnp.clip(values, -48.0, 48.0).astype(jnp.bfloat16)


def draw_encodings(key, part):
    values = jnp.clip(jax.random.normal(jax.random.fold_in(key, 506), (BLOCKS, NTOK, E), jnp.float32), -6.0, 6.0)
    return jnp.clip(values, -12.0, 12.0).astype(jnp.bfloat16)


def draw_neighbour_ids(key, part):
    return neighbour_plan(key)[0]


def draw_block_place(key, part):
    return neighbour_plan(key)[1]


def draw_query_weight(key, part):
    return projections(key)[0].astype(jnp.bfloat16)


def draw_key_weight(key, part):
    return projections(key)[1].astype(jnp.bfloat16)


def levels(rng, extent, cuts, smallest, high):
    def one(axis_at, shards_of):
        draws = jax.random.uniform(jax.random.fold_in(jax.random.fold_in(rng, 6), axis_at), (shards_of,), jnp.float32, smallest / len(cuts), high / len(cuts))
        return jnp.repeat(jnp.exp(draws), extent[axis_at] // shards_of).reshape((-1,) + (1,) * (len(extent) - axis_at - 1))

    level = one(*cuts[0])
    for cut in cuts[1:]:
        level = level * one(*cut)
    return level


def gaussian(key, extent, scale, most, shards=(), dtype=jnp.bfloat16):
    values = scale * jax.random.normal(key, extent, jnp.float32)
    if shards:
        values = values * levels(key, extent, shards, -0.22, 0.18)
    return jnp.clip(values, -most, most).astype(dtype)


def setup_inputs(seed: int = 0) -> dict:
    key_list = jax.random.split(jax.random.key(seed), 9)
    queries = draw_queries(jax.random.fold_in(key_list[8], 71), 0)
    encodings = draw_encodings(jax.random.fold_in(key_list[8], 71), 0)
    neighbour_ids = draw_neighbour_ids(jax.random.fold_in(key_list[8], 71), 0)
    block_place = draw_block_place(jax.random.fold_in(key_list[8], 71), 0)
    query_weight = draw_query_weight(jax.random.fold_in(key_list[8], 71), 0)
    key_weight = draw_key_weight(jax.random.fold_in(key_list[8], 71), 0)
    value_weight = gaussian(key_list[6], (E, HC), E ** -0.5, 0.1875, ((1, 4),))
    attn_grad = gaussian(key_list[7], (TOKENS, HC), 4.0, 24.0, ((0, 64), (1, 4)))
    return dict(queries=queries, encodings=encodings, neighbour_ids=neighbour_ids, block_place=block_place, query_weight=query_weight, key_weight=key_weight, value_weight=value_weight, attn_grad=attn_grad)


def span_grads(parts):
    query_rows = parts[0].astype(jnp.float32)
    key_rows = parts[1].astype(jnp.float32)
    value_rows = parts[2].astype(jnp.float32)
    grad_rows = parts[3].astype(jnp.float32)
    score_scale = 1.0 / math.sqrt(DH)
    scores = jnp.einsum('qhd,khd->hqk', query_rows, key_rows) * score_scale
    shifted = jnp.exp(scores - lax.optimization_barrier(jnp.max(scores, axis=-1, keepdims=True)))
    prob_rows = shifted / lax.optimization_barrier(jnp.sum(shifted, axis=-1, keepdims=True))
    prob_half = lax.optimization_barrier(prob_rows.astype(jnp.bfloat16)).astype(jnp.float32)
    grad_probs = jnp.einsum('qhd,khd->hqk', grad_rows, value_rows)
    row_delta = lax.optimization_barrier(jnp.sum(prob_rows * grad_probs, axis=-1, keepdims=True))
    grad_scores = (prob_rows * (grad_probs - row_delta) * score_scale).astype(jnp.bfloat16)
    grad_scores = lax.optimization_barrier(grad_scores).astype(jnp.float32)
    value_grad = jnp.einsum('hqk,qhd->khd', prob_half, grad_rows).astype(jnp.bfloat16)
    key_grad = jnp.einsum('hqk,qhd->khd', grad_scores, query_rows).astype(jnp.bfloat16)
    query_grad = jnp.einsum('hqk,khd->qhd', grad_scores, key_rows).astype(jnp.bfloat16)
    return (query_grad, key_grad, value_grad)

def reference(queries, encodings, neighbour_ids, block_place, query_weight, key_weight, value_weight, attn_grad):
    position = block_place[neighbour_ids.reshape(-1)].astype(jnp.int32)
    blocks = encodings[position]
    flat_rows = blocks.reshape(-1, E)
    keys = jnp.dot(flat_rows, key_weight, preferred_element_type=jnp.float32).astype(jnp.bfloat16)
    values = jnp.dot(flat_rows, value_weight, preferred_element_type=jnp.float32).astype(jnp.bfloat16)
    query_heads = queries.reshape(SPANS, CH, HEADS, DH)
    key_heads = keys.reshape(SPANS, NEIGH * NTOK, HEADS, DH)
    value_heads = values.reshape(SPANS, NEIGH * NTOK, HEADS, DH)
    grad_heads = attn_grad.reshape(SPANS, CH, HEADS, DH)
    query_grad, key_grad, value_grad = lax.map(span_grads, (query_heads, key_heads, value_heads, grad_heads))
    query_grad = query_grad.reshape(TOKENS, HC)
    key_flat = key_grad.reshape(-1, HC)
    value_flat = value_grad.reshape(-1, HC)
    group_cols = HC // N_HEAD
    input_total = jnp.zeros((TOKENS, D), jnp.float32)
    slot_total = jnp.zeros((flat_rows.shape[0], E), jnp.float32)
    for group in range(N_HEAD):
        low = group * group_cols
        high = low + group_cols
        query_part = jnp.dot(query_grad[:, low:high], query_weight[:, low:high].T, preferred_element_type=jnp.float32)
        input_total = input_total + query_part.astype(jnp.bfloat16).astype(jnp.float32)
        slot_part = jnp.dot(key_flat[:, low:high], key_weight[:, low:high].T, preferred_element_type=jnp.float32)
        slot_part = slot_part + jnp.dot(value_flat[:, low:high], value_weight[:, low:high].T, preferred_element_type=jnp.float32)
        slot_total = slot_total + slot_part.astype(jnp.bfloat16).astype(jnp.float32)
    query_input_grad = input_total.astype(jnp.bfloat16)
    key_weight_grad = jnp.dot(flat_rows.T, key_flat, preferred_element_type=jnp.float32)
    value_weight_grad = jnp.dot(flat_rows.T, value_flat, preferred_element_type=jnp.float32)
    slot_grad = slot_total.astype(jnp.bfloat16).reshape(NEIGH * SPANS, NTOK, E)
    summed = jnp.zeros((BLOCKS, NTOK, E), jnp.float32).at[position].add(slot_grad.astype(jnp.float32))
    return (query_input_grad, summed.astype(jnp.bfloat16), key_weight_grad, value_weight_grad)
```

```python
import math

import jax
import jax.numpy as jnp
from jax import lax
from jax.experimental import pallas as pl
from jax.experimental.pallas import tpu as pltpu
from jax.sharding import Mesh, PartitionSpec as P

DH = 128
CH = 64
NTOK = 128
NEIGH = 2
BF = jnp.bfloat16
F32 = jnp.float32
DP = ("z", "x", "c")
SPLITS = (112, 112)


def nt(a, b):
    return lax.dot_general(a, b, (((1,), (1,)), ((), ())), preferred_element_type=F32)


def nn(a, b):
    return jnp.dot(a, b, preferred_element_type=F32)


def span_kernel(heads, head_count, quarter, splits, head_ref, *refs):
    n = len(splits)
    pieces = [refs[5 * i : 5 * i + 5] for i in range(n)]
    wt, w, q, g, qt, gt = refs[5 * n : 5 * n + 6]
    slot_out = refs[5 * n + 6 : 6 * n + 6]
    bgt, xt, qg = refs[6 * n + 6 :]
    span = pl.program_id(0)
    half = pl.num_programs(0) // 2
    me = head_ref[0]
    left = lax.rem(me + head_count - 1, head_count)
    right = lax.rem(me + 1, head_count)
    across = lax.rem(me + 2, head_count)

    def put(owner, offset, rows, ref):
        start = pl.multiple_of(owner * quarter + offset, 16)
        for s in range(NEIGH):
            xt[pl.ds(start, rows), s * NTOK : (s + 1) * NTOK] = ref[s]

    offset = 0
    for (own, from_left, from_right, far_low, far_high), rows in zip(pieces, splits):
        put(me, offset, rows, own)
        put(left, offset, rows, from_left)
        put(right, offset, rows, from_right)

        @pl.when(span < half)
        def _(offset=offset, rows=rows, ref=far_low):
            put(across, offset, rows, ref)

        @pl.when(span >= half)
        def _(offset=offset, rows=rows, ref=far_high):
            put(across, offset, rows, ref)

        offset += rows

    kvt = nn(wt[...], xt[...]).astype(BF)
    scale = 1.0 / math.sqrt(DH)
    cols = heads * DH
    for h in range(heads):
        lo, hi = h * DH, (h + 1) * DH
        kt = kvt[lo:hi]
        vt = kvt[cols + lo : cols + hi]
        scores = nn(q[:, lo:hi], kt) * scale
        dprobs = nn(g[:, lo:hi], vt)
        e = jnp.exp(scores - jnp.max(scores, axis=1, keepdims=True))
        probs = e / jnp.sum(e, axis=1, keepdims=True)
        delta = jnp.sum(probs * dprobs, axis=1, keepdims=True)
        ds = (probs * (dprobs - delta) * scale).astype(BF)
        ph = probs.astype(BF)
        bgt[lo:hi, :] = nn(qt[0, lo:hi, :], ds).astype(BF)
        bgt[cols + lo : cols + hi, :] = nn(gt[0, lo:hi, :], ph).astype(BF)
        qg[:, lo:hi] = nt(ds, kt).astype(BF)
    slot = nn(w[...], bgt[...]).astype(BF)
    for j in range(head_count):
        offset = j * quarter
        for out, rows in zip(slot_out, splits):
            for s in range(NEIGH):
                out[j, s] = slot[offset : offset + rows, s * NTOK : (s + 1) * NTOK]
            offset += rows


def span_call(head_id, pieces, wt, w, q, g, qt, gt, head_count):
    splits = [p[0].shape[1] for p in pieces]
    quarter = sum(splits)
    slots = pieces[0][0].shape[0]
    spans = slots // NEIGH
    half = spans // 2
    cols = q.shape[1]
    e = w.shape[0]
    in_specs = []
    for rows in splits:
        block = (NEIGH, rows, NTOK)
        in_specs += [pl.BlockSpec(block, lambda i, h: (i, 0, 0))] * 3
        in_specs.append(pl.BlockSpec(block, lambda i, h: (jnp.minimum(i, half - 1), 0, 0)))
        in_specs.append(pl.BlockSpec(block, lambda i, h: (jnp.maximum(i - half, 0), 0, 0)))
    whole = lambda a: pl.BlockSpec(a.shape, lambda i, h: (0,) * a.ndim)
    row = pl.BlockSpec((CH, cols), lambda i, h: (i, 0))
    turned = pl.BlockSpec((1, cols, CH), lambda i, h: (i, 0, 0))
    in_specs += [whole(wt), whole(w), row, row, turned, turned]
    out_shape = [jax.ShapeDtypeStruct((head_count, slots, rows, NTOK), BF) for rows in splits]
    out_specs = [
        pl.BlockSpec((head_count, NEIGH, rows, NTOK), lambda i, h: (0, i, 0, 0)) for rows in splits
    ]
    keys = NEIGH * NTOK
    for rows in (2 * cols, e):
        out_shape.append(jax.ShapeDtypeStruct((rows, slots * NTOK), BF))
        out_specs.append(pl.BlockSpec((rows, keys), lambda i, h: (0, i)))
    out_shape.append(jax.ShapeDtypeStruct(q.shape, BF))
    out_specs.append(row)

    def body(*refs):
        span_kernel(cols // DH, head_count, quarter, splits, *refs)

    flat = [a for p in pieces for a in p]
    outs = pl.pallas_call(
        body,
        grid_spec=pltpu.PrefetchScalarGridSpec(
            num_scalar_prefetch=1, grid=(spans,), in_specs=in_specs, out_specs=out_specs
        ),
        out_shape=out_shape,
        name="span_grads",
    )(head_id, *flat, wt, w, q, g, qt, gt)
    n = len(splits)
    return outs[:n], outs[n], outs[n + 1], outs[n + 2]


def sum_kernel(idx_ref, valid_ref, r, *rest):
    out, acc = rest[-2], rest[-1]
    acc[...] = jnp.zeros_like(acc)

    def step(o, carry):
        @pl.when(valid_ref[o] > 0)
        def _():
            b = idx_ref[o]
            acc[b] = acc[b] + r[o].astype(F32)

        return carry

    lax.fori_loop(0, r.shape[0], step, 0)
    out[...] = acc[...].astype(BF)


def sum_call(idx, valid, returned, own_blocks, quarter, offset, so_far):
    rows = returned.shape[1]
    step = 16
    base = offset // step
    in_specs = [pl.BlockSpec((returned.shape[0], step, NTOK), lambda i, a, b: (0, i, 0))]
    args = [idx, valid, returned]
    aliases = {}
    if so_far is not None:
        in_specs.append(pl.BlockSpec(memory_space=pl.ANY))
        args.append(so_far)
        aliases = {3: 0}
    return pl.pallas_call(
        sum_kernel,
        grid_spec=pltpu.PrefetchScalarGridSpec(
            num_scalar_prefetch=2,
            grid=(rows // step,),
            in_specs=in_specs,
            out_specs=pl.BlockSpec((own_blocks, step, NTOK), lambda i, a, b: (0, base + i, 0)),
            scratch_shapes=[pltpu.VMEM((own_blocks, step, NTOK), F32)],
        ),
        out_shape=jax.ShapeDtypeStruct((own_blocks, quarter, NTOK), BF),
        input_output_aliases=aliases,
        name="block_sums",
    )(*args)


def rows_at(a, index):
    return a.at[index].get(mode="promise_in_bounds")


def shards(queries, encodings, neighbour_ids, block_place, query_weight, key_weight, value_weight, attn_grad):
    dp_count = lax.axis_size("z") * lax.axis_size("x") * lax.axis_size("c")
    head_count = lax.axis_size("head")
    own_blocks, _, quarter = encodings.shape
    slots = neighbour_ids.size
    cols = key_weight.shape[1]
    head_id = lax.axis_index("head").astype(jnp.int32).reshape(1)

    position = rows_at(block_place, neighbour_ids.reshape(-1))
    owner = position // own_blocks
    local = position % own_blocks
    match = owner[:, None] == jnp.arange(dp_count, dtype=jnp.int32)[None, :]
    requests = jnp.sum(jnp.where(match, local[:, None] + 1, 0), axis=0) - 1
    slot_of = jnp.sum(
        jnp.where(match, jnp.arange(slots, dtype=jnp.int32)[:, None], 0), axis=0
    )
    asked = lax.all_to_all(requests.reshape(dp_count, 1, 1), DP, 0, 0, tiled=True).reshape(-1)
    index = jnp.maximum(asked, 0)
    valid = (asked >= 0).astype(jnp.int32)

    stored = jnp.swapaxes(encodings, 1, 2)
    up = [(i, (i + 1) % head_count) for i in range(head_count)]
    down = [(i, (i - 1) % head_count) for i in range(head_count)]
    pieces = []
    offset = 0
    for rows in SPLITS:
        packed = rows_at(stored[:, offset : offset + rows], index)
        received = lax.all_to_all(packed, DP, 0, 0, tiled=True)
        own = rows_at(received, owner)
        from_left = lax.ppermute(own, "head", up)
        from_right = lax.ppermute(own, "head", down)
        far_low = lax.ppermute(from_left[: slots // 2], "head", up)
        far_high = lax.ppermute(from_right[slots // 2 :], "head", down)
        pieces.append((own, from_left, from_right, far_low, far_high))
        offset += rows

    w = jnp.concatenate([key_weight, value_weight], axis=1)
    spans = slots // NEIGH
    qt = queries.reshape(spans, CH, cols).swapaxes(1, 2)
    gt = attn_grad.reshape(spans, CH, cols).swapaxes(1, 2)
    slot_parts, bgt, xt, query_grad = span_call(
        head_id, pieces, w.T, w, queries, attn_grad, qt, gt, head_count
    )

    encodings_grad = None
    offset = 0
    returned = []
    for part in slot_parts:
        parts = lax.all_to_all(part, "head", 0, 0, tiled=True)
        slot_grad = jnp.sum(parts.astype(F32), axis=0).astype(BF)
        returned.append(lax.all_to_all(rows_at(slot_grad, slot_of), DP, 0, 0, tiled=True))
    for part in returned:
        encodings_grad = sum_call(index, valid, part, own_blocks, quarter, offset, encodings_grad)
        offset += part.shape[1]

    weight_part = nt(xt, bgt)
    e = weight_part.shape[0]
    chips = dp_count // 2
    by_core = weight_part.reshape(chips, 2, e // dp_count, 2 * cols)
    core = lax.axis_index("c")
    mine = lax.dynamic_index_in_dim(by_core, core, 1, keepdims=False)
    other = lax.dynamic_index_in_dim(by_core, 1 - core, 1, keepdims=False)
    pair = mine + lax.ppermute(other, "c", [(0, 1), (1, 0)])
    spread = lax.all_to_all(pair.astype(BF), ("z", "x"), 0, 0, tiled=True)
    weight_grad = jnp.sum(spread.astype(F32), axis=0)

    width = query_weight.shape[0] // head_count
    query_parts = jnp.stack(
        [nt(query_grad, query_weight[j * width : (j + 1) * width]).astype(BF) for j in range(head_count)]
    )
    query_parts = lax.all_to_all(query_parts, "head", 0, 0, tiled=True)
    query_input_grad = jnp.sum(query_parts.astype(F32), axis=0).astype(BF)

    return (
        query_input_grad,
        jnp.swapaxes(encodings_grad, 1, 2),
        weight_grad[:, :cols],
        weight_grad[:, cols:],
    )


def solution(mesh):
    dp, head = mesh.devices.shape
    fine = Mesh(mesh.devices.reshape(dp // 8, 4, 2, head), ("z", "x", "c", "head"))
    in_specs = (
        P(DP, "head"),
        P(DP, None, "head"),
        P(DP, None),
        P(),
        P(None, "head"),
        P(None, "head"),
        P(None, "head"),
        P(DP, "head"),
    )
    out_specs = (P(DP, "head"), P(DP, None, "head"), P(DP, "head"), P(DP, "head"))
    return jax.shard_map(shards, mesh=fine, in_specs=in_specs, out_specs=out_specs, check_vma=False)
```

```python
import math

import jax
import jax.numpy as jnp
from jax import lax
from jax.experimental import pallas as pl
from jax.experimental.pallas import tpu as pltpu
from jax.sharding import Mesh, PartitionSpec as P

DH = 128
CH = 64
NTOK = 128
NEIGH = 2
BF = jnp.bfloat16
F32 = jnp.float32
DP = ("z", "x", "c")
SPLITS_IN = (160, 64)
SPLITS_OUT = (64, 160)
GROUP = 2


def nt(a, b):
    return lax.dot_general(a, b, (((1,), (1,)), ((), ())), preferred_element_type=F32)


def nn(a, b):
    return jnp.dot(a, b, preferred_element_type=F32)


def span_kernel(heads, head_count, quarter, splits_in, splits_out, head_ref, *refs):
    n, m = len(splits_in), len(splits_out)
    pieces = [refs[4 * i : 4 * i + 4] for i in range(n)]
    wt, w, q, g, qt, gt = refs[4 * n : 4 * n + 6]
    outs = refs[4 * n + 6 :]
    slot_out = [outs[4 * i : 4 * i + 4] for i in range(m)]
    bgt, xt, qg = outs[4 * m :]
    me = head_ref[0]
    order = (
        me,
        lax.rem(me + 1, head_count),
        lax.rem(me + head_count - 1, head_count),
        lax.rem(me + 2, head_count),
    )

    slots = GROUP * NEIGH
    offset = 0
    for piece, rows in zip(pieces, splits_in):
        for ref, owner in zip(piece, order):
            start = pl.multiple_of(owner * quarter + offset, 16)
            for s in range(slots):
                xt[pl.ds(start, rows), s * NTOK : (s + 1) * NTOK] = ref[s]
        offset += rows

    kvt = nn(wt[...], xt[...]).astype(BF)
    scale = 1.0 / math.sqrt(DH)
    cols = heads * DH
    keys = NEIGH * NTOK
    cuts = [(c, h * DH, c * CH, c * keys) for c in range(GROUP) for h in range(heads)]
    kts = [kvt[lo : lo + DH, at : at + keys] for c, lo, row, at in cuts]
    scores = [nn(q[row : row + CH, lo : lo + DH], kt) * scale for (c, lo, row, at), kt in zip(cuts, kts)]
    dprobs = [
        nn(g[row : row + CH, lo : lo + DH], kvt[cols + lo : cols + lo + DH, at : at + keys])
        for c, lo, row, at in cuts
    ]
    half, dscores = [], []
    for s, d in zip(scores, dprobs):
        e = jnp.exp(s - jnp.max(s, axis=1, keepdims=True))
        probs = e * (1.0 / jnp.sum(e, axis=1, keepdims=True))
        delta = jnp.sum(probs * d, axis=1, keepdims=True)
        half.append(probs.astype(BF))
        dscores.append((probs * (d - delta) * scale).astype(BF))
    for (c, lo, row, at), kt, ph, ds in zip(cuts, kts, half, dscores):
        bgt[lo : lo + DH, at : at + keys] = nn(qt[c, lo : lo + DH, :], ds).astype(BF)
        bgt[cols + lo : cols + lo + DH, at : at + keys] = nn(gt[c, lo : lo + DH, :], ph).astype(BF)
        qg[row : row + CH, lo : lo + DH] = nt(ds, kt).astype(BF)
    both = bgt[...]
    for j, dest in enumerate(order):
        part = w[pl.ds(pl.multiple_of(dest * quarter, 16), quarter), :]
        slot = nn(part, both).astype(BF)
        offset = 0
        for out, rows in zip(slot_out, splits_out):
            for s in range(slots):
                out[j][s] = slot[offset : offset + rows, s * NTOK : (s + 1) * NTOK]
            offset += rows


def span_call(head_id, pieces, wt, w, q, g, qt, gt, head_count, splits_out):
    splits_in = [p[0].shape[1] for p in pieces]
    quarter = sum(splits_in)
    slots = pieces[0][0].shape[0]
    spans = slots // NEIGH
    cols = q.shape[1]
    e = w.shape[0]
    block = lambda rows: pl.BlockSpec((GROUP * NEIGH, rows, NTOK), lambda i, h: (i, 0, 0))
    whole = lambda a: pl.BlockSpec(a.shape, lambda i, h: (0,) * a.ndim)
    row = pl.BlockSpec((GROUP * CH, cols), lambda i, h: (i, 0))
    turned = pl.BlockSpec((GROUP, cols, CH), lambda i, h: (i, 0, 0))
    in_specs = [block(rows) for rows in splits_in for _ in range(head_count)]
    in_specs += [whole(wt), whole(w), row, row, turned, turned]
    out_shape, out_specs = [], []
    for rows in splits_out:
        out_shape += [jax.ShapeDtypeStruct((slots, rows, NTOK), BF)] * head_count
        out_specs += [block(rows)] * head_count
    keys = GROUP * NEIGH * NTOK
    for rows in (2 * cols, e):
        out_shape.append(jax.ShapeDtypeStruct((rows, slots * NTOK), BF))
        out_specs.append(pl.BlockSpec((rows, keys), lambda i, h: (0, i)))
    out_shape.append(jax.ShapeDtypeStruct(q.shape, BF))
    out_specs.append(row)

    def body(*refs):
        span_kernel(cols // DH, head_count, quarter, splits_in, splits_out, *refs)

    flat = [a for p in pieces for a in p]
    outs = pl.pallas_call(
        body,
        grid_spec=pltpu.PrefetchScalarGridSpec(
            num_scalar_prefetch=1, grid=(spans // GROUP,), in_specs=in_specs, out_specs=out_specs
        ),
        out_shape=out_shape,
        name="span_grads",
    )(head_id, *flat, wt, w, q, g, qt, gt)
    m = len(splits_out)
    slot_parts = [outs[4 * i : 4 * i + 4] for i in range(m)]
    return slot_parts, outs[4 * m], outs[4 * m + 1], outs[4 * m + 2]


def head_sum(parts, up, down, across):
    own, to_right, to_left, to_across = parts
    got = (
        lax.ppermute(to_right, "head", up),
        lax.ppermute(to_left, "head", down),
        lax.ppermute(to_across, "head", across),
    )
    total = own.astype(F32)
    for p in got:
        total = total + p.astype(F32)
    return total.astype(BF)


def halve(a, axis, name, bit):
    size = lax.axis_size(name)
    side = (lax.axis_index(name) // bit) % 2
    mine = lax.dynamic_index_in_dim(a, side, axis, keepdims=False)
    other = lax.dynamic_index_in_dim(a, 1 - side, axis, keepdims=False)
    return mine + lax.ppermute(other, name, [(i, i ^ bit) for i in range(size)])


def sum_kernel(idx_ref, valid_ref, r, *rest):
    out, acc = rest[-2], rest[-1]
    acc[...] = jnp.zeros_like(acc)

    def step(o, carry):
        @pl.when(valid_ref[o] > 0)
        def _():
            b = idx_ref[o]
            acc[b] = acc[b] + r[o].astype(F32)

        return carry

    lax.fori_loop(0, r.shape[0], step, 0)

    offset = 0
    for done in rest[:-2]:
        out[:, : done.shape[1]] = done[...]
        offset += done.shape[1]
    out[:, offset:] = acc[...].astype(BF)


def sum_call(idx, valid, returned, own_blocks, done=()):
    rows = returned.shape[1]
    total = rows + sum(d.shape[1] for d in done)
    return pl.pallas_call(
        sum_kernel,
        grid_spec=pltpu.PrefetchScalarGridSpec(
            num_scalar_prefetch=2,
            grid=(1,),
            in_specs=[pl.BlockSpec(a.shape, lambda i, x, v: (0, 0, 0)) for a in (returned, *done)],
            out_specs=pl.BlockSpec((own_blocks, total, NTOK), lambda i, x, v: (0, 0, 0)),
            scratch_shapes=[pltpu.VMEM((own_blocks, rows, NTOK), F32)],
        ),
        out_shape=jax.ShapeDtypeStruct((own_blocks, total, NTOK), BF),
        name="block_sums",
    )(idx, valid, returned, *done)


def rows_at(a, index):
    return a.at[index].get(mode="promise_in_bounds")


def shards(queries, encodings, neighbour_ids, block_place, query_weight, key_weight, value_weight, attn_grad):
    dp_count = lax.axis_size("z") * lax.axis_size("x") * lax.axis_size("c")
    head_count = lax.axis_size("head")
    own_blocks, _, quarter = encodings.shape
    slots = neighbour_ids.size
    cols = key_weight.shape[1]
    head_id = lax.axis_index("head").astype(jnp.int32).reshape(1)

    position = rows_at(block_place, neighbour_ids.reshape(-1))
    owner = position // own_blocks
    local = position % own_blocks
    match = owner[:, None] == jnp.arange(dp_count, dtype=jnp.int32)[None, :]
    requests = jnp.sum(jnp.where(match, local[:, None] + 1, 0), axis=0) - 1
    slot_of = jnp.sum(
        jnp.where(match, jnp.arange(slots, dtype=jnp.int32)[:, None], 0), axis=0
    )
    asked = lax.all_to_all(requests.reshape(dp_count, 1, 1), DP, 0, 0, tiled=True).reshape(-1)
    index = jnp.maximum(asked, 0)
    valid = (asked >= 0).astype(jnp.int32)

    stored = jnp.swapaxes(encodings, 1, 2)
    up = [(i, (i + 1) % head_count) for i in range(head_count)]
    down = [(i, (i - 1) % head_count) for i in range(head_count)]
    across = [(i, (i + 2) % head_count) for i in range(head_count)]
    pieces = []
    offset = 0
    for rows in SPLITS_IN:
        packed = rows_at(stored[:, offset : offset + rows], index)
        received = lax.all_to_all(packed, DP, 0, 0, tiled=True)
        own = rows_at(received, owner)
        from_right = lax.ppermute(own, "head", down)
        from_left = lax.ppermute(own, "head", up)
        from_across = lax.ppermute(own, "head", across)
        pieces.append((own, from_right, from_left, from_across))
        offset += rows

    w = jnp.concatenate([key_weight, value_weight], axis=1)
    spans = slots // NEIGH
    qt = queries.reshape(spans, CH, cols).swapaxes(1, 2)
    gt = attn_grad.reshape(spans, CH, cols).swapaxes(1, 2)
    slot_parts, bgt, xt, query_grad = span_call(
        head_id, pieces, w.T, w, queries, attn_grad, qt, gt, head_count, SPLITS_OUT
    )

    returned = []
    for part in slot_parts:
        slot_grad = head_sum(part, up, down, across)
        returned.append(lax.all_to_all(rows_at(slot_grad, slot_of), DP, 0, 0, tiled=True))
    done = sum_call(index, valid, returned[0], own_blocks)
    encodings_grad = sum_call(index, valid, returned[1], own_blocks, (done,))

    weight_part = nt(xt, bgt)
    e = weight_part.shape[0]
    x_size, z_size = lax.axis_size("x"), lax.axis_size("z")
    dims = (2,) * (z_size.bit_length() - 1 + x_size.bit_length() - 1 + 1)
    total = weight_part.reshape(*dims, e // dp_count, 2 * cols)
    total = halve(total, len(dims) - 1, "c", 1)
    total = halve(total, 3, "x", 2)
    total = halve(total, 3, "x", 1)
    total = halve(total, 0, "z", 4)
    total = halve(total, 0, "z", 2)
    weight_grad = halve(total, 0, "z", 1)

    width = query_weight.shape[0] // head_count
    me = head_id[0]
    query_parts = []
    for dest in (me, (me + 1) % head_count, (me + 3) % head_count, (me + 2) % head_count):
        part = lax.dynamic_slice_in_dim(query_weight, dest * width, width, 0)
        query_parts.append(nt(query_grad, part).astype(BF))
    query_input_grad = head_sum(query_parts, up, down, across)

    return (
        query_input_grad,
        jnp.swapaxes(encodings_grad, 1, 2),
        weight_grad[:, :cols],
        weight_grad[:, cols:],
    )


def solution(mesh):
    dp, head = mesh.devices.shape
    fine = Mesh(mesh.devices.reshape(dp // 8, 4, 2, head), ("z", "x", "c", "head"))
    in_specs = (
        P(DP, "head"),
        P(DP, None, "head"),
        P(DP, None),
        P(),
        P(None, "head"),
        P(None, "head"),
        P(None, "head"),
        P(DP, "head"),
    )
    out_specs = (P(DP, "head"), P(DP, None, "head"), P(DP, "head"), P(DP, "head"))
    return jax.shard_map(shards, mesh=fine, in_specs=in_specs, out_specs=out_specs, check_vma=False)
```
